256 devices in a mesh: seg: 4 (over y), bond: 64 (over z, x, core).
Axes of the slice: x: 4, y: 4, z: 8, core: 2. Of those that a mesh axis runs over, the one named last changes fastest.
Arguments:
- sites: float32 [4, 2, 8192, 8192], P('seg', None, 'bond'), may hold values from -0.6629126 to 0.6629126, as said below
- boundary: float32 [8192], P('bond'), may hold values from -6 to 6
- bits: int32 [32, 4], P(None, 'seg'), may hold values from 0 to 1
- order: int32 [32], replicated, may hold values from 0 to 31, each once
Outputs:
- probs: float32 [32, 4], P(None, 'seg')
The draws below stay inside these ranges and needn't reach their ends.
Inputs may be any that keep to these rules, and one draw needn't show every extreme that they name: `order`: each slot number appears once. `sites`: real entries.
All inputs are finite; a program needn't handle non-finite values.
Results may differ from the reference program's by a relative error of at most 0.0001.
Values sent between devices are 32-bit elements; how exact they have to be, the bound alone decides.
A program may use at most 64 MiB of HBM per device.

```python
import math
import jax
import jax.numpy as jnp
from jax import lax

D = 8192
ROWS = 32
SITES = 4


def draw_sites(key, part):
    noise_key = jax.random.fold_in(key, 11)
    row_key = jax.random.fold_in(key, 23)
    col_key = jax.random.fold_in(key, 37)
    shape = (SITES, 2, D, D)
    noise = jax.random.truncated_normal(noise_key, -6.0, 6.0, shape, jnp.float32)
    row_scale = jnp.exp(jax.random.uniform(row_key, (SITES, 2, D, 1), jnp.float32, 0.0, math.log(10.0)))
    col_scale = jnp.exp(jax.random.uniform(col_key, (SITES, 2, 1, D), jnp.float32, 0.0, math.log(10.0)))
    return noise * row_scale * col_scale * (0.1 / math.sqrt(D))


def with_ends(array, stream_key, low, top_value):
    longest = array.shape.index(max(array.shape))
    spots = []
    for shift in (0, 1):
        where = [jax.random.randint(jax.random.fold_in(stream_key, axis), (), 0, length) for axis, length in enumerate(array.shape)]
        where[longest] = (where[longest] + shift) % array.shape[longest]
        spots.append(tuple(where))
    return array.at[spots[0]].set(low).at[spots[1]].set(top_value)


def block_scale(key, shape, cuts, smallest, top_value):
    def one(position, blocks):
        steps = jax.random.uniform(jax.random.fold_in(jax.random.fold_in(key, 6), position), (blocks,), jnp.float32, smallest / len(cuts), top_value / len(cuts))
        return jnp.repeat(jnp.exp(steps), shape[position] // blocks).reshape((-1,) + (1,) * (len(shape) - position - 1))

    factor_of = one(*cuts[0])
    for cut in cuts[1:]:
        factor_of = factor_of * one(*cut)
    return factor_of


def scatter_about(key, dims, width, bound, cuts=(), dtype=jnp.bfloat16):
    values = width * jax.random.normal(key, dims, jnp.float32)
    if cuts:
        values = values * block_scale(key, dims, cuts, -0.22, 0.18)
    return jnp.clip(values, -bound, bound).astype(dtype)


def setup_inputs(seed: int = 0) -> dict:
    arg_keys = jax.random.split(jax.random.key(seed), 5)
    sites = draw_sites(jax.random.fold_in(arg_keys[4], 71), 0)
    boundary = scatter_about(arg_keys[1], (D,), 1.0, 6.0, ((0, 64),), jnp.float32)
    bits = with_ends(jax.random.randint(arg_keys[2], (ROWS, SITES), 0, 2), jax.random.fold_in(arg_keys[2], 1), 0, 1).astype(jnp.int32)
    order = jax.random.permutation(arg_keys[3], ROWS).astype(jnp.int32)
    return dict(sites=sites, boundary=boundary, bits=bits, order=order)


EPSILON = 1e-06

def reference(sites, boundary, bits, order):
    slot_bits = jnp.take(bits, order, axis=0)
    env = jnp.broadcast_to(boundary[None, :], (ROWS, D)).astype(jnp.float32)
    columns = []
    for k in range(SITES):
        amp_zero = jnp.dot(env, sites[k, 0], precision=lax.Precision.HIGHEST, preferred_element_type=jnp.float32)
        amp_one = jnp.dot(env, sites[k, 1], precision=lax.Precision.HIGHEST, preferred_element_type=jnp.float32)
        mean_zero = lax.optimization_barrier(jnp.mean(amp_zero * amp_zero, axis=1)) + EPSILON
        mean_one = lax.optimization_barrier(jnp.mean(amp_one * amp_one, axis=1)) + EPSILON
        picked = slot_bits[:, k] == 1
        weight = jnp.where(picked, mean_one, mean_zero)
        columns.append(weight / (mean_zero + mean_one))
        chosen = jnp.where(picked[:, None], amp_one, amp_zero)
        env = chosen * lax.rsqrt(weight)[:, None]
    return jnp.stack(columns, axis=1)
```

```python
import functools

import jax
import jax.numpy as jnp
from jax import lax
from jax.experimental import pallas as pl
from jax.experimental.pallas import tpu as pltpu
from jax.sharding import PartitionSpec as P

EPSILON = 1e-06
LANES = 128
SEGS = 4
MXU_FROM = 2


def grouping(bonds):
    ng = 8 if bonds == 64 else 2
    return bonds // ng, ng


def group_orders(ng):
    nx = ng // 2
    far = sorted(range(nx), key=lambda d: -min(d, nx - d))
    pairs = [(dx, dc) for dx in far if dx for dc in (0, 1)]
    return pairs + [(0, 1), (0, 0)]


def ring_order(n):
    return sorted(range(n), key=lambda d: -min(d, n - d))


def lookup(t, table):
    value = jnp.int32(table[0])
    for i, entry in enumerate(table):
        if i:
            value = jnp.where(t == i, jnp.int32(entry), value)
    return value


def lane_iota(rows):
    return lax.broadcasted_iota(jnp.int32, (rows, LANES), 1)


def row_iota(rows):
    return lax.broadcasted_iota(jnp.int32, (rows, LANES), 0)


def column_of(row, rows):
    hit = lane_iota(rows) == row_iota(rows)
    zero = jnp.zeros((), row.dtype)
    return jnp.sum(jnp.where(hit, jnp.broadcast_to(row, (rows, LANES)), zero), axis=1, keepdims=True)


def row_of(column, offset):
    rows = column.shape[0]
    hit = lane_iota(rows) == row_iota(rows) + offset
    return jnp.sum(jnp.where(hit, jnp.broadcast_to(column, (rows, LANES)), 0.0), axis=0, keepdims=True)


def level_offset(k):
    return 2 ** (k + 1) - 2


def kernel(
    nz, ng, slots, dim,
    sites, boundary, bits, order, out,
    tile, split, envs,
    pa0, pa1, pa2, pa3, ra0, ra1, ra2, ra3,
    pb0, pb1, pb2, pb3, rb0, rb1, rb2, rb3,
    pe2, pe3, re2, re3,
    fs, fr, s1, r1, s2, r2,
    load_sem, sa_sem, ra_sem, sb_sem, rb_sem, se_sem, re_sem, rb3_sem, re3_sem, f_sem, fr_sem, s1_sem, r1_sem, s2_sem, r2_sem,
):
    pa, ra = (pa0, pa1, pa2, pa3), (ra0, ra1, ra2, ra3)
    pb, rb = (pb0, pb1, pb2, pb3), (rb0, rb1, rb2, rb3)
    pe, re = (None, None, pe2, pe3), (None, None, re2, re3)
    last = SEGS - 1
    seg, bond = lax.axis_index("seg"), lax.axis_index("bond")
    z_me, g_me = lax.div(bond, ng), lax.rem(bond, ng)
    x_me, c_me = lax.div(g_me, 2), lax.rem(g_me, 2)
    pairs = group_orders(ng)
    bonds = nz * ng
    width = tile.shape[2]

    def member(dx, dc):
        return lax.rem(x_me + dx, ng // 2) * 2 + lax.rem(c_me + dc, 2)

    def remote(src, dst, send, recv, to_seg, to_bond):
        return pltpu.make_async_remote_copy(
            src_ref=src, dst_ref=dst, send_sem=send, recv_sem=recv,
            device_id={"seg": to_seg, "bond": to_bond}, device_id_type=pl.DeviceIdType.MESH,
        )

    def wait_bytes(ref, sem):
        pltpu.make_async_copy(ref, ref, sem).wait()

    def load(t):
        g = member(lookup(t, [p[0] for p in pairs]), lookup(t, [p[1] for p in pairs]))
        for z in range(nz):
            start = pl.multiple_of((z * ng + g) * width, width)
            pltpu.make_async_copy(
                sites.at[0, :, :, pl.ds(start, width)],
                tile.at[g, :, :, pl.ds(z * width, width)],
                load_sem.at[t],
            ).start()

    pl.loop(0, ng)(load)

    barrier = pltpu.get_barrier_semaphore()

    def hello(to_seg, to_bond):
        pl.semaphore_signal(
            barrier, inc=1, device_id={"seg": to_seg, "bond": to_bond}, device_id_type=pl.DeviceIdType.MESH
        )

    for dx, dc in pairs[:-1]:
        hello(seg, z_me * ng + member(dx, dc))

    @pl.when(seg > 0)
    def _():
        for d in ring_order(nz):
            hello(seg - 1, lax.rem(z_me + d, nz) * ng + g_me)

    @pl.when(seg == last)
    def _():
        for d in ring_order(nz)[:-1]:
            hello(seg, lax.rem(z_me + d, nz) * ng + g_me)

    @pl.when(seg < last)
    def _():
        hello(last, bond)

    bits_row = row_of(bits[...].astype(jnp.float32), 0)
    order_column = column_of(order[...], slots)

    def group_of(t):
        dx, dc = lookup(t, [p[0] for p in pairs]), lookup(t, [p[1] for p in pairs])
        return member(dx, dc), dx * 2 + dc - 1

    def wait_tile(t, g):
        wait_bytes(tile.at[g], load_sem.at[t])

    @pl.when(seg >= MXU_FROM)
    def _():
        @pl.loop(0, ng)
        def _(t):
            g, _slot = group_of(t)
            wait_tile(t, g)
            for s in range(2):
                a = tile[g, s]
                high = a.astype(jnp.bfloat16)
                low = (a - high.astype(jnp.float32)).astype(jnp.bfloat16)
                span = pl.ds(s * nz * width, nz * width)
                split[g, 0:width, span] = high
                split[g, width : 2 * width, span] = low

    @pl.when(seg < last)
    def _():
        pl.semaphore_wait(barrier, ng - 1 + nz)

    @pl.when(seg == last)
    def _():
        pl.semaphore_wait(barrier, ng - 1 + nz - 1 + last)

    def probabilities(totals, row_bits):
        lanes = lane_iota(slots)
        table = jnp.broadcast_to(totals, (slots, LANES))
        node = jnp.zeros((slots, 1), jnp.int32)
        scale = jnp.full((slots, 1), float(dim), jnp.float32)
        answer = jnp.zeros((slots, 1), jnp.float32)

        def pick(where_lane, source):
            return jnp.sum(jnp.where(lanes == where_lane, source, 0.0), axis=1, keepdims=True)

        for k in range(SEGS):
            if k < last:
                bit = pick(order_column + (32 + slots * k), table)
            else:
                bit = pick(order_column, jnp.broadcast_to(row_bits, (slots, LANES)))
            chosen = (bit > 0.5).astype(jnp.int32)
            base = level_offset(k) + node
            m_chosen = pick(base + chosen * 2**k, table) / scale + EPSILON
            m_other = pick(base + (1 - chosen) * 2**k, table) / scale + EPSILON
            answer = jnp.where(seg == k, m_chosen / (m_chosen + m_other), answer)
            scale = scale * m_chosen
            node = node + chosen * 2**k
        return answer

    for k in range(SEGS):
        rows_in = 2**k
        rows_out = 2 * rows_in
        embed = pe[k] is None

        @pl.when(seg == k)
        def _(k=k, rows_in=rows_in, rows_out=rows_out, embed=embed):
            if k == 0:
                env = boundary[...]
                extra = row_of(bits[...].astype(jnp.float32), 32) / bonds
            else:
                source = rb[k - 1]
                wait_bytes(source, rb_sem)
                env = source[0, 0:rows_in, :]
                for d in range(1, nz):
                    env = env + source[d, 0:rows_in, :]
                if pe[k - 1] is None:
                    extra = source[0, rows_in : rows_in + 1, :]
                    for d in range(1, nz):
                        extra = extra + source[d, rows_in : rows_in + 1, :]
                else:
                    wait_bytes(re[k - 1], re_sem)
                    extra = re[k - 1][0]
                    for d in range(1, nz):
                        extra = extra + re[k - 1][d]
                extra = extra / bonds + row_of(jnp.sum(env * env, axis=1, keepdims=True), level_offset(k - 1))
                if k < last:
                    extra = extra + row_of(bits[...].astype(jnp.float32), 32 + slots * k) / bonds

            if k < MXU_FROM:
                for j in range(rows_in):
                    envs[j] = jnp.broadcast_to(column_of(env[j : j + 1, :], width), (width, width))
            else:
                if rows_in < 8:
                    env = jnp.concatenate([env, jnp.zeros((8 - rows_in, width), jnp.float32)], axis=0)
                high = env.astype(jnp.bfloat16).astype(jnp.float32)
                both = jnp.concatenate([high, env - high], axis=0).astype(jnp.bfloat16)
                left = jnp.concatenate([both, both], axis=1)
            extra8 = jnp.broadcast_to(extra, (8, LANES))

            @pl.loop(0, ng)
            def _(t):
                g, slot = group_of(t)
                if k < MXU_FROM:
                    wait_tile(t, g)
                    for z in range(nz):
                        for s in range(2):
                            a = tile[g, s, :, z * width : (z + 1) * width]
                            for j in range(rows_in):
                                row = z * rows_out + s * rows_in + j
                                pa[k][g, row : row + 1, :] = jnp.sum(a * envs[j], axis=0, keepdims=True)
                else:
                    product = jnp.dot(left, split[g], preferred_element_type=jnp.float32)
                    product = product[0:8] + product[8:16]
                    for z in range(nz):
                        for s in range(2):
                            row = z * rows_out + s * rows_in
                            column = (s * nz + z) * width
                            pa[k][g, row : row + rows_in, :] = product[0:rows_in, column : column + width]
                pa[k][g, nz * rows_out : nz * rows_out + 8, :] = extra8

                @pl.when(t < ng - 1)
                def _():
                    remote(pa[k].at[g], ra[k].at[slot], sa_sem, ra_sem, seg, z_me * ng + g).start()

            wait_bytes(ra[k], ra_sem)
            for z in range(nz):
                rows = slice(z * rows_out, (z + 1) * rows_out)
                total = pa[k][g_me, rows, :]
                for i in range(ng - 1):
                    total = total + ra[k][i, rows, :]
                pb[k][z, 0:rows_out, :] = total
            rows = slice(nz * rows_out, nz * rows_out + 8)
            total = pa[k][g_me, rows, :]
            for i in range(ng - 1):
                total = total + ra[k][i, rows, :]
            if embed:
                for z in range(nz):
                    pb[k][z, rows_out : 2 * rows_out, :] = total[0:rows_out]
            else:
                pe[k][...] = total[0:1]

            to_seg = seg + 1 if k < last else seg
            data_sem, extra_sem = (rb_sem, re_sem) if k < last else (rb3_sem, re3_sem)
            for d in ring_order(nz):
                if k == last and d == 0:
                    continue
                z = lax.rem(z_me + d, nz)
                slot = d if k < last else d - 1
                to_bond = z * ng + g_me
                remote(pb[k].at[z], rb[k].at[slot], sb_sem, data_sem, to_seg, to_bond).start()
                if not embed:
                    remote(pe[k], re[k].at[slot], se_sem, extra_sem, to_seg, to_bond).start()

            if k < last:
                wait_bytes(fr, fr_sem)
                out[...] = probabilities(fr[...], bits_row)
            else:
                wait_bytes(rb[k], rb3_sem)
                final = pb[k][z_me]
                for d in range(nz - 1):
                    final = final + rb[k][d]
                s1[...] = row_of(jnp.sum(final * final, axis=1, keepdims=True), level_offset(k))
                for dx, dc in pairs[:-1]:
                    remote(
                        s1, r1.at[dx * 2 + dc - 1], s1_sem, r1_sem, seg, z_me * ng + member(dx, dc)
                    ).start()
                wait_bytes(re[k], re3_sem)
                known = pe[k][...]
                for d in range(nz - 1):
                    known = known + re[k][d]
                fs[...] = known
                for to in range(last):
                    remote(fs, fr, f_sem, fr_sem, to, bond).start()
                wait_bytes(r1, r1_sem)
                norms = s1[...]
                for i in range(ng - 1):
                    norms = norms + r1[i]
                s2[...] = norms
                for d in ring_order(nz)[:-1]:
                    z = lax.rem(z_me + d, nz)
                    remote(s2, r2.at[d - 1], s2_sem, r2_sem, seg, z * ng + g_me).start()
                wait_bytes(r2, r2_sem)
                for d in range(nz - 1):
                    norms = norms + r2[d]
                out[...] = probabilities(known + norms, bits_row)
                wait_bytes(r1, s1_sem)
                wait_bytes(r2, s2_sem)
                for _i in range(last):
                    wait_bytes(fs, f_sem)

            wait_bytes(ra[k], sa_sem)
            wait_bytes(rb[k], sb_sem)
            if not embed:
                wait_bytes(re[k], se_sem)


def on_device(nz, ng, sites, boundary, bits, order):
    slots = bits.shape[0]
    width = sites.shape[2]
    dim = sites.shape[3]
    f32 = jnp.float32

    def rows(k):
        return 2 ** (k + 1)

    pa = [pltpu.VMEM((ng, nz * rows(k) + 8, LANES), f32) for k in range(SEGS)]
    ra = [pltpu.VMEM((ng - 1, nz * rows(k) + 8, LANES), f32) for k in range(SEGS)]
    held = [rows(k) * (2 if k < 2 else 1) for k in range(SEGS)]
    pb = [pltpu.VMEM((nz, held[k], LANES), f32) for k in range(SEGS)]
    rb = [pltpu.VMEM((nz if k < SEGS - 1 else nz - 1, held[k], LANES), f32) for k in range(SEGS)]
    one = pltpu.VMEM((1, LANES), f32)
    dma = pltpu.SemaphoreType.DMA
    scratch = [
        pltpu.VMEM((ng, 2, width, nz * width), f32),
        pltpu.VMEM((ng, 2 * width, 2 * nz * width), jnp.bfloat16),
        pltpu.VMEM((2, width, LANES), f32),
        *pa, *ra, *pb, *rb,
        one, one,
        pltpu.VMEM((nz, 1, LANES), f32), pltpu.VMEM((nz - 1, 1, LANES), f32),
        one, one,
        one, pltpu.VMEM((ng - 1, 1, LANES), f32),
        one, pltpu.VMEM((nz - 1, 1, LANES), f32),
        dma((ng,)),
        *([dma(())] * 14),
    ]
    padded = jnp.pad(order, (0, LANES - slots)).reshape(1, LANES)
    vmem = pl.BlockSpec(memory_space=pltpu.VMEM)
    return pl.pallas_call(
        functools.partial(kernel, nz, ng, slots, dim),
        out_shape=jax.ShapeDtypeStruct((slots, 1), f32),
        in_specs=[pl.BlockSpec(memory_space=pl.ANY), vmem, vmem, vmem],
        out_specs=vmem,
        scratch_shapes=scratch,
        compiler_params=pltpu.CompilerParams(
            collective_id=0, has_side_effects=True, vmem_limit_bytes=48 * 1024 * 1024
        ),
        name="chain",
    )(sites, boundary.reshape(1, width), bits, padded)


def solution(mesh):
    nz, ng = grouping(mesh.shape["bond"])
    return jax.shard_map(
        functools.partial(on_device, nz, ng),
        mesh=mesh,
        in_specs=(P("seg", None, "bond", None), P("bond"), P(None, "seg"), P()),
        out_specs=P(None, "seg"),
        check_vma=False,
    )
```

```python
import functools

import jax
import jax.numpy as jnp
from jax import lax
from jax.experimental import pallas as pl
from jax.experimental.pallas import tpu as pltpu
from jax.sharding import PartitionSpec as P

EPSILON = 1e-06
LANES = 128
SEGS = 4
MESH = pl.DeviceIdType.MESH


def grouping(bonds):
    return (8, 4) if bonds == 64 else (bonds // 2, 1)


def far_first(n):
    return sorted(range(n), key=lambda d: -min(d, n - d))


def lookup(t, table):
    value = jnp.int32(table[0])
    for i, entry in enumerate(table):
        if i:
            value = jnp.where(t == i, jnp.int32(entry), value)
    return value


def iota(shape, axis):
    return lax.broadcasted_iota(jnp.int32, shape, axis)


def column_of(row, rows):
    shape = (rows, row.shape[1])
    hit = iota(shape, 1) == iota(shape, 0)
    zero = jnp.zeros((), row.dtype)
    return jnp.sum(jnp.where(hit, jnp.broadcast_to(row, shape), zero), axis=1, keepdims=True)


def row_of(column, offset, lanes=LANES):
    shape = (column.shape[0], lanes)
    hit = iota(shape, 1) == iota(shape, 0) + offset
    return jnp.sum(jnp.where(hit, jnp.broadcast_to(column, shape), 0.0), axis=0, keepdims=True)


def total_of(ref, count, rows):
    chains = [ref[i, rows, :] for i in range(min(4, count))]
    for i in range(4, count):
        chains[i % 4] = chains[i % 4] + ref[i, rows, :]
    while len(chains) > 1:
        chains = [sum(chains[i + 1 : i + 2], chains[i]) for i in range(0, len(chains), 2)]
    return chains[0]


def level_offset(k):
    return 2 ** (k + 1) - 2


def kernel(
    nz, nx, slots, dim,
    sites, boundary_hbm, bits_hbm, order_hbm, out,
    tile, split, env0, boundary, bits, order,
    pp1, pp2, pp3, rp1, rp2, rp3,
    pb0, pb1, pb2, pb3, rb0, rb1, rb2, rb3,
    fs, fr, s1, r1,
    load_sem, small_sem, sp_sem, rp_sem, sb_sem, rb_sem, rb3_sem, f_sem, fr_sem, s1_sem, r1_sem,
):
    pp, rp = (None, pp1, pp2, pp3), (None, rp1, rp2, rp3)
    pb, rb = (pb0, pb1, pb2, pb3), (rb0, rb1, rb2, rb3)
    last = SEGS - 1
    bonds, ng = nz * nx * 2, nx * 2
    width = tile.shape[2]
    seg, bond = lax.axis_index("seg"), lax.axis_index("bond")
    z_me, g_me = lax.div(bond, ng), lax.rem(bond, ng)
    x_me, c_me = lax.div(g_me, 2), lax.rem(g_me, 2)
    partner = lax.rem(c_me + 1, 2)
    xs = far_first(nx)
    chips = [(dz, dx) for dz in far_first(nz) for dx in xs]

    def at(dz, dx, core):
        return (lax.rem(z_me + dz, nz) * nx + lax.rem(x_me + dx, nx)) * 2 + core

    def remote(src, dst, send, recv, to_seg, to_bond):
        return pltpu.make_async_remote_copy(
            src_ref=src, dst_ref=dst, send_sem=send, recv_sem=recv,
            device_id={"seg": to_seg, "bond": to_bond}, device_id_type=MESH,
        )

    def wait_bytes(ref, sem):
        pltpu.make_async_copy(ref, ref, sem).wait()

    barrier = pltpu.get_barrier_semaphore()

    def hello(to_seg, to_bond):
        pl.semaphore_signal(barrier, inc=1, device_id={"seg": to_seg, "bond": to_bond}, device_id_type=MESH)

    @pl.when(seg == 1)
    def _():
        for dz, dx in chips:
            for core in (0, 1):
                hello(0, at(dz, dx, core))

    @pl.when(seg >= 2)
    def _():
        for dz, dx in chips:
            hello(seg - 1, at(dz, dx, c_me))

    @pl.when(seg == last)
    def _():
        for dz, dx in chips:
            hello(seg, at(dz, dx, partner))
            if dz or dx:
                hello(seg, at(dz, dx, c_me))

    @pl.when(seg < last)
    def _():
        hello(last, bond)

    @pl.when(jnp.logical_and(seg > 0, seg < last))
    def _():
        hello(seg, at(0, 0, partner))

    small = [
        pltpu.make_async_copy(src, dst, small_sem.at[i])
        for i, (src, dst) in enumerate(((boundary_hbm, boundary), (bits_hbm, bits), (order_hbm, order)))
    ]
    for copy in small:
        copy.start()

    def piece(t):
        dx = lookup(t, xs + xs)
        return lax.rem(x_me + dx, nx) * 2 + jnp.where(t < nx, partner, c_me)

    @pl.loop(0, ng)
    def _(t):
        g = piece(t)
        for z in range(nz):
            start = pl.multiple_of((z * ng + g) * width, width)
            pltpu.make_async_copy(
                sites.at[0, :, :, pl.ds(start, width)],
                tile.at[g, :, :, pl.ds(z * width, width)],
                load_sem.at[t],
            ).start()

    for copy in small:
        copy.wait()
    bits_row = bits[...].astype(jnp.float32)
    order_column = column_of(order[...], slots)

    def bits_at(k):
        parts = [jnp.zeros((1, slots), jnp.float32)] * (LANES // slots)
        parts[k + 1] = bits_row
        return jnp.concatenate(parts, axis=1)

    @pl.when(seg == 0)
    def _():
        extra = bits_at(0) / bonds
        env0[...] = jnp.broadcast_to(column_of(boundary[...], width), (width, LANES))

        @pl.loop(0, ng)
        def _(t):
            g = piece(t)
            wait_bytes(tile.at[g], load_sem.at[t])
            for z in range(nz):
                for s in range(2):
                    a = tile[g, s, :, z * width : (z + 1) * width]
                    pb0[g * nz + z, s : s + 1, :] = jnp.sum(a * env0[...], axis=0, keepdims=True)
                pb0[g * nz + z, 2:3, :] = extra

    @pl.when(seg > 0)
    def _():
        @pl.loop(0, ng)
        def _(t):
            g = piece(t)
            wait_bytes(tile.at[g], load_sem.at[t])
            for s in range(2):
                a = tile[g, s]
                high = a.astype(jnp.bfloat16)
                low = (a - high.astype(jnp.float32)).astype(jnp.bfloat16)
                span = pl.ds(s * nz * width, nz * width)
                split[g, 0:width, span] = high
                split[g, width : 2 * width, span] = low

    @pl.when(seg == 0)
    def _():
        pl.semaphore_wait(barrier, bonds)

    @pl.when(jnp.logical_and(seg > 0, seg < last))
    def _():
        pl.semaphore_wait(barrier, 1 + nz * nx)

    @pl.when(seg == last)
    def _():
        pl.semaphore_wait(barrier, bonds - 1 + last)

    lanes = iota((slots, LANES), 1)

    def pick(where_lane, source):
        return jnp.sum(jnp.where(lanes == where_lane, source, 0.0), axis=1, keepdims=True)

    def site_probability(k, table, bit, node, scale):
        chosen = (bit > 0.5).astype(jnp.int32)
        base = level_offset(k) + node
        m_chosen = pick(base + chosen * 2**k, table) / scale + EPSILON
        m_other = pick(base + (1 - chosen) * 2**k, table) / scale + EPSILON
        return m_chosen / (m_chosen + m_other), node + chosen * 2**k, scale * m_chosen

    def early_sites(known):
        table = jnp.broadcast_to(known, (slots, LANES))
        state = (jnp.zeros((slots, 1), jnp.int32), jnp.full((slots, 1), float(dim), jnp.float32))
        answer = jnp.zeros((slots, 1), jnp.float32)
        for k in range(last):
            bit = pick(order_column + slots * (k + 1), table)
            probability, *state = site_probability(k, table, bit, *state)
            answer = jnp.where(seg == k, probability, answer)
        return answer, state

    def receive(k):
        count = bonds if k == 1 else nz * nx
        rows = 2**k
        wait_bytes(rb[k - 1], rb_sem)
        env = total_of(rb[k - 1], count, slice(0, rows))
        extra = total_of(rb[k - 1], count, slice(rows, rows + 1)) / bonds
        return env, extra

    def advance(k):
        rows_in, rows_out = 2**k, 2 ** (k + 1)
        block = nz * rows_out
        env, extra = receive(k)
        env8 = env
        if rows_in < 8:
            env8 = jnp.concatenate([env, jnp.zeros((8 - rows_in, width), jnp.float32)], axis=0)
        high = env8.astype(jnp.bfloat16).astype(jnp.float32)
        both = jnp.concatenate([high, env8 - high], axis=0).astype(jnp.bfloat16)
        left = jnp.concatenate([both, both], axis=1)
        extra = extra + row_of(jnp.sum(env * env, axis=1, keepdims=True), level_offset(k - 1))
        if k < last:
            extra = extra + bits_at(k) / bonds

        def product(x, core):
            value = jnp.dot(left, split[x * 2 + core], preferred_element_type=jnp.float32)
            return value[0:8] + value[8:16]

        for t, dx in enumerate(xs):
            x = lax.rem(x_me + dx, nx)
            value = product(x, partner)
            for z in range(nz):
                for s in range(2):
                    row, column = z * rows_out + s * rows_in, (s * nz + z) * width
                    pp[k][t, row : row + rows_in, :] = value[0:rows_in, column : column + width]
            pp[k][t, block : block + 8, :] = jnp.broadcast_to(extra, (8, LANES))
            remote(pp[k].at[t], rp[k].at[t], sp_sem, rp_sem.at[t], seg, at(0, 0, partner)).start()

        to_seg = seg + 1 if k < last else seg
        recv = rb_sem if k < last else rb3_sem
        for t, dx in enumerate(xs):
            x = lax.rem(x_me + dx, nx)
            value = product(x, c_me)
            wait_bytes(rp[k].at[t], rp_sem.at[t])
            if t == 0:
                extra = extra + rp[k][t, block : block + 1, :]
            for z in range(nz):
                for s in range(2):
                    row, column = z * rows_out + s * rows_in, (s * nz + z) * width
                    pb[k][t * nz + z, s * rows_in : (s + 1) * rows_in, :] = (
                        value[0:rows_in, column : column + width] + rp[k][t, row : row + rows_in, :]
                    )
                pb[k][t * nz + z, rows_out : rows_out + 1, :] = extra
            for dz in far_first(nz):
                if k == last and dz == 0 and dx == 0:
                    continue
                slot = dz * nx + dx - (1 if k == last else 0)
                z = lax.rem(z_me + dz, nz)
                remote(pb[k].at[t * nz + z], rb[k].at[slot], sb_sem, recv, to_seg, at(dz, dx, c_me)).start()

    def drain(k):
        if k:
            wait_bytes(rp[k], sp_sem)
        wait_bytes(rb[k], sb_sem)

    @pl.when(seg == 0)
    def _():
        for dz, dx in chips:
            for core in (0, 1):
                to = at(dz, dx, core)
                mine = lax.rem(to, ng) * nz + lax.div(to, ng)
                remote(pb0.at[mine], rb0.at[(dz * nx + dx) * 2 + lax.rem(c_me + core, 2)], sb_sem, rb_sem, 1, to).start()

    for k in range(1, SEGS):
        pl.when(seg == k)(functools.partial(advance, k))

    @pl.when(seg < last)
    def _():
        wait_bytes(fr, fr_sem)
        answer, _state = early_sites(fr[...])
        out[...] = row_of(answer, 0, slots)

    for k in range(last):
        pl.when(seg == k)(functools.partial(drain, k))

    @pl.when(seg == last)
    def _():
        k, rows = last, 2 ** (last + 1)
        own = xs.index(0) * nz + z_me
        wait_bytes(rb[k], rb3_sem)
        env = pb[k][own, 0:rows, :] + total_of(rb[k], nz * nx - 1, slice(0, rows))
        s1[...] = row_of(jnp.sum(env * env, axis=1, keepdims=True), level_offset(k))
        for dz, dx in chips:
            for dc in (1, 0):
                if dz or dx or dc:
                    core = lax.rem(c_me + dc, 2)
                    remote(s1, r1.at[(dz * nx + dx) * 2 + dc - 1], s1_sem, r1_sem, seg, at(dz, dx, core)).start()
        known = pb[k][own, rows : rows + 1, :] + total_of(rb[k], nz * nx - 1, slice(rows, rows + 1))
        fs[...] = known
        for to in range(last):
            remote(fs, fr, f_sem, fr_sem, to, bond).start()
        _answer, state = early_sites(known)
        bit = pick(order_column, jnp.concatenate([bits_row] * (LANES // slots), axis=1))
        wait_bytes(r1, r1_sem)
        norms = s1[...] + total_of(r1, bonds - 1, slice(0, 1))
        probability, *_state = site_probability(k, jnp.broadcast_to(norms, (slots, LANES)), bit, *state)
        out[...] = row_of(probability, 0, slots)
        wait_bytes(r1, s1_sem)
        for _i in range(last):
            wait_bytes(fs, f_sem)
        drain(k)


def on_device(nz, nx, sites, boundary, bits, order):
    slots = bits.shape[0]
    width, dim = sites.shape[2], sites.shape[3]
    f32, i32 = jnp.float32, jnp.int32
    bonds, ng = nz * nx * 2, nx * 2
    rows = [2 ** (k + 1) for k in range(SEGS)]
    pieces = [pltpu.VMEM((nx, nz * rows[k] + 8, LANES), f32) for k in range(1, SEGS)]
    sends = [pltpu.VMEM((nz * nx * (1 if k else 2), rows[k] + 1, LANES), f32) for k in range(SEGS)]
    counts = [bonds, nz * nx, nz * nx, nz * nx - 1]
    receives = [pltpu.VMEM((counts[k], rows[k] + 1, LANES), f32) for k in range(SEGS)]
    one = pltpu.VMEM((1, LANES), f32)
    dma = pltpu.SemaphoreType.DMA
    scratch = [
        pltpu.VMEM((ng, 2, width, nz * width), f32),
        pltpu.VMEM((ng, 2 * width, 2 * nz * width), jnp.bfloat16),
        pltpu.VMEM((width, LANES), f32),
        pltpu.VMEM((1, width), f32), pltpu.VMEM((1, slots), i32), pltpu.VMEM((1, slots), i32),
        *pieces, *pieces, *sends, *receives,
        one, one, one, pltpu.VMEM((bonds - 1, 1, LANES), f32),
        dma((ng,)), dma((3,)), dma(()), dma((nx,)), *([dma(())] * 7),
    ]
    hbm = pl.BlockSpec(memory_space=pltpu.HBM)
    answer = pl.pallas_call(
        functools.partial(kernel, nz, nx, slots, dim),
        out_shape=jax.ShapeDtypeStruct((1, slots), f32),
        in_specs=[hbm] * 4,
        out_specs=pl.BlockSpec(memory_space=pltpu.VMEM),
        scratch_shapes=scratch,
        compiler_params=pltpu.CompilerParams(
            collective_id=0, has_side_effects=True, vmem_limit_bytes=67043328
        ),
        name="chain",
    )(sites, boundary.reshape(1, width), bits.T, order.reshape(1, slots))
    return answer.T


def solution(mesh):
    nz, nx = grouping(mesh.shape["bond"])
    return jax.shard_map(
        functools.partial(on_device, nz, nx),
        mesh=mesh,
        in_specs=(P("seg", None, "bond", None), P("bond"), P(None, "seg"), P()),
        out_specs=P(None, "seg"),
        check_vma=False,
    )
```

```python
import functools

import jax
import jax.numpy as jnp
from jax import lax
from jax.experimental import pallas as pl
from jax.experimental.pallas import tpu as pltpu
from jax.sharding import PartitionSpec as P

EPSILON = 1e-06
LANES = 128
SEGS = 4
MESH = pl.DeviceIdType.MESH
UNMERGED = (8, 3, 1, 0)


def grouping(bonds):
    return (8, 4) if bonds == 64 else (bonds // 2, 1)


def far_first(n):
    return sorted(range(n), key=lambda d: -min(d, n - d))


def unmerged(k, nz):
    return min(UNMERGED[k], nz - 1) if k else nz


def sources(k, nz, nx):
    direct = far_first(nz)[: unmerged(k, nz)]
    listed = [
        (dz, dx, dc) for dz in far_first(nz) for dx in far_first(nx) for dc in ((1, 0) if dz in direct else (0,))
    ]
    if k == SEGS - 1:
        listed.remove((0, 0, 0))
    return listed


def iota(shape, axis):
    return lax.broadcasted_iota(jnp.int32, shape, axis)


def column_of(row, rows):
    shape = (rows, row.shape[1])
    hit = iota(shape, 1) == iota(shape, 0)
    zero = jnp.zeros((), row.dtype)
    return jnp.sum(jnp.where(hit, jnp.broadcast_to(row, shape), zero), axis=1, keepdims=True)


def row_of(column, offset, lanes=LANES):
    shape = (column.shape[0], lanes)
    hit = iota(shape, 1) == iota(shape, 0) + offset
    return jnp.sum(jnp.where(hit, jnp.broadcast_to(column, shape), 0.0), axis=0, keepdims=True)


def total_of(ref, count, rows):
    chains = [ref[i, rows, :] for i in range(min(4, count))]
    for i in range(4, count):
        chains[i % 4] = chains[i % 4] + ref[i, rows, :]
    while len(chains) > 1:
        chains = [sum(chains[i + 1 : i + 2], chains[i]) for i in range(0, len(chains), 2)]
    return chains[0]


def level_offset(k):
    return 2 ** (k + 1) - 2


def kernel(
    nz, nx, slots, dim,
    sites, boundary_hbm, bits_hbm, order_hbm, out,
    tile, split, env0, boundary, bits, order,
    pp1, pp2, pp3, rp1, rp2, rp3,
    pb0, pb1, pb2, pb3, rb0, rb1, rb2, rb3,
    note, notes, fs, fr, s0, r0, s1, r1,
    load_sem, small_sem, notes_sem, rp_sem, note_sem, sp_sem, sb_sem, rb_sem, rb3_sem, f_sem, fr_sem,
    s0_sem, r0_sem, s1_sem, r1_sem,
):
    pp, rp = (None, pp1, pp2, pp3), (None, rp1, rp2, rp3)
    pb, rb = (pb0, pb1, pb2, pb3), (rb0, rb1, rb2, rb3)
    last = SEGS - 1
    bonds, ng = nz * nx * 2, nx * 2
    width = tile.shape[2]
    seg, bond = lax.axis_index("seg"), lax.axis_index("bond")
    z_me, g_me = lax.div(bond, ng), lax.rem(bond, ng)
    x_me, c_me = lax.div(g_me, 2), lax.rem(g_me, 2)
    partner = lax.rem(c_me + 1, 2)
    xs = far_first(nx)
    chips = [(dz, dx) for dz in far_first(nz) for dx in xs]

    def at(dz, dx, core):
        return (lax.rem(z_me + dz, nz) * nx + lax.rem(x_me + dx, nx)) * 2 + core

    def remote(src, dst, send, recv, to_seg, to_bond):
        return pltpu.make_async_remote_copy(
            src_ref=src, dst_ref=dst, send_sem=send, recv_sem=recv,
            device_id={"seg": to_seg, "bond": to_bond}, device_id_type=MESH,
        )

    def wait_bytes(ref, sem):
        pltpu.make_async_copy(ref, ref, sem).wait()

    barrier = pltpu.get_barrier_semaphore()

    def hello(to_seg, to_bond):
        pl.semaphore_signal(barrier, inc=1, device_id={"seg": to_seg, "bond": to_bond}, device_id_type=MESH)

    for k in range(1, SEGS):
        @pl.when(seg == k)
        def _(k=k):
            for dz, dx, dc in sources(k - 1, nz, nx):
                hello(k - 1, at(dz, dx, lax.rem(c_me + dc, 2)))

    everyone = [(dz, dx, dc) for dz, dx in chips for dc in (1, 0) if dz or dx or dc]

    @pl.when(seg == last)
    def _():
        for dz, dx, dc in everyone:
            hello(seg, at(dz, dx, lax.rem(c_me + dc, 2)))
        for k in range(last - 1):
            hello(k, bond)

    @pl.when(seg < last)
    def _():
        hello(last, bond)

    @pl.when(jnp.logical_and(seg > 0, seg < last))
    def _():
        hello(seg, at(0, 0, partner))

    small = [
        pltpu.make_async_copy(src, dst, small_sem.at[i])
        for i, (src, dst) in enumerate(((boundary_hbm, boundary), (bits_hbm, bits), (order_hbm, order)))
    ]
    for copy in small:
        copy.start()

    zs = far_first(nz)

    @pl.loop(0, nz)
    def _(z):
        start = pl.multiple_of(z * ng * width, width)
        pltpu.make_async_copy(sites.at[0, :, :, pl.ds(start, ng * width)], tile.at[z], load_sem.at[z]).start()

    for copy in small:
        copy.wait()
    bits_row = bits[...].astype(jnp.float32)
    order_column = column_of(order[...], slots)

    def bits_at(k):
        parts = [jnp.zeros((1, slots), jnp.float32)] * (LANES // slots)
        parts[k + 1] = bits_row
        return jnp.concatenate(parts, axis=1)

    @pl.when(seg == 0)
    def _():
        env0[...] = jnp.broadcast_to(column_of(boundary[...], width), (width, LANES))

        @pl.loop(0, nz)
        def _(z):
            wait_bytes(tile.at[z], load_sem.at[z])
            for g in range(ng):
                for s in range(2):
                    a = tile[z, s, :, g * width : (g + 1) * width]
                    pb0[z * ng + g, s : s + 1, :] = jnp.sum(a * env0[...], axis=0, keepdims=True)

    @pl.when(seg > 0)
    def _():
        @pl.loop(0, nz)
        def _(z):
            wait_bytes(tile.at[z], load_sem.at[z])
            for s in range(2):
                for g in range(ng):
                    x, core = g // 2, g % 2
                    a = tile[z, s, :, g * width : (g + 1) * width]
                    high = a.astype(jnp.bfloat16)
                    low = (a - high.astype(jnp.float32)).astype(jnp.bfloat16)
                    column = (s * nx + x) * width
                    split[z, core, 0:width, column : column + width] = high
                    split[z, core, width : 2 * width, column : column + width] = low

    for k in range(SEGS):
        @pl.when(seg == k)
        def _(k=k):
            if k == last:
                count = len(everyone) + last
            else:
                count = len(sources(k, nz, nx)) + (1 if k > 0 else 0) + (1 if k < last - 1 else 0)
            pl.semaphore_wait(barrier, count)

    lanes = iota((slots, LANES), 1)

    def pick(where_lane, source):
        return jnp.sum(jnp.where(lanes == where_lane, source, 0.0), axis=1, keepdims=True)

    def site_probability(k, table, bit, node, scale):
        chosen = (bit > 0.5).astype(jnp.int32)
        base = level_offset(k) + node
        m_chosen = pick(base + chosen * 2**k, table) / scale + EPSILON
        m_other = pick(base + (1 - chosen) * 2**k, table) / scale + EPSILON
        return m_chosen / (m_chosen + m_other), node + chosen * 2**k, scale * m_chosen

    def early_sites(known):
        table = jnp.broadcast_to(known, (slots, LANES))
        state = (jnp.zeros((slots, 1), jnp.int32), jnp.full((slots, 1), float(dim), jnp.float32))
        answer = jnp.zeros((slots, 1), jnp.float32)
        for k in range(last):
            bit = pick(order_column + slots * (k + 1), table)
            probability, *state = site_probability(k, table, bit, *state)
            answer = jnp.where(seg == k, probability, answer)
        return answer, state

    def receive(k):
        wait_bytes(rb[k - 1], rb_sem)
        return total_of(rb[k - 1], len(sources(k - 1, nz, nx)), slice(0, 2**k))

    def norm_row(env, k):
        return row_of(jnp.sum(env * env, axis=1, keepdims=True), level_offset(k))

    def report(k, row):
        note[...] = row
        remote(note, notes.at[k], note_sem, notes_sem.at[k], last, bond).start()

    def advance(k):
        rows_in, rows_out = 2**k, 2 ** (k + 1)
        env = receive(k)
        env8 = env
        if rows_in < 8:
            env8 = jnp.concatenate([env, jnp.zeros((8 - rows_in, width), jnp.float32)], axis=0)
        high = env8.astype(jnp.bfloat16).astype(jnp.float32)
        both = jnp.concatenate([high, env8 - high], axis=0).astype(jnp.bfloat16)
        left = jnp.concatenate([both, both], axis=1)
        to_seg, recv = (seg + 1, rb_sem) if k < last else (seg, rb3_sem)
        slot_of = {source: i for i, source in enumerate(sources(k, nz, nx))}

        def blocks(t, core):
            z = lax.rem(z_me + zs[t], nz)
            value = jnp.dot(left, split[z, core], preferred_element_type=jnp.float32)
            value = value[0:8] + value[8:16]
            for x in range(nx):
                for s in range(2):
                    column = (s * nx + x) * width
                    yield x, s * rows_in, value[0:rows_in, column : column + width]

        def to_partner(t, products):
            for x, row, value in products:
                row = x * rows_out + row
                pp[k][t, row : row + rows_in, :] = value
            remote(pp[k].at[t], rp[k].at[t], sp_sem, rp_sem.at[t], seg, at(0, 0, partner)).start()

        def send(t, dc, piece_at):
            for dx in xs:
                source = (zs[t], dx, dc)
                if source in slot_of:
                    x = lax.rem(x_me + dx, nx)
                    to = at(zs[t], dx, lax.rem(c_me + dc, 2))
                    remote(pb[k].at[piece_at + x], rb[k].at[slot_of[source]], sb_sem, recv, to_seg, to).start()

        def own(t, products):
            wait_bytes(rp[k].at[t], rp_sem.at[t])
            for x, row, value in products:
                sent = x * rows_out + row
                pb[k][t * nx + x, row : row + rows_in, :] = value + rp[k][t, sent : sent + rows_in, :]
            send(t, 0, t * nx)

        def direct(dc, t, products):
            piece_at = (t + dc * nz) * nx
            for x, row, value in products:
                pb[k][piece_at + x, row : row + rows_in, :] = value
            send(t, dc, piece_at)

        def norms_ahead(_t, _products):
            share = norm_row(env, k - 1)
            for i in range(last):
                wait_bytes(notes.at[i], notes_sem.at[i])
                share = share + notes[i]
            s0[...] = share
            to_everyone(s0, r0, s0_sem, r0_sem)

        far = unmerged(k, nz)
        both_cores = [(functools.partial(direct, dc), t, (c_me, partner)[dc]) for t in range(far) for dc in (1, 0)]
        exchanged = [(to_partner, t, partner) for t in range(far, nz)]
        steps = both_cores[:2] + exchanged[:2] + both_cores[2:] + exchanged[2:]
        if k == last:
            steps.append((norms_ahead, 0, None))
        steps += [(own, t, c_me) for t in range(far, nz)]
        held = None
        for finish, t, core in steps:
            products = [] if core is None else list(blocks(t, core))
            if held is not None:
                held[0](*held[1:])
            held = (finish, t, products)
        held[0](*held[1:])
        if k < last:
            report(k, norm_row(env, k - 1) + bits_at(k))

    def to_everyone(src, dst, send, recv):
        for i, (dz, dx, dc) in enumerate(everyone):
            remote(src, dst.at[i], send, recv, seg, at(dz, dx, lax.rem(c_me + dc, 2))).start()

    def drain(k):
        if k:
            far = unmerged(k, nz)
            wait_bytes(rp[k].at[pl.ds(far, nz - far)], sp_sem)
        wait_bytes(rb[k], sb_sem)
        if k < last:
            wait_bytes(note, note_sem)

    @pl.when(seg == 0)
    def _():
        for i, (dz, dx, dc) in enumerate(sources(0, nz, nx)):
            to = at(dz, dx, lax.rem(c_me + dc, 2))
            remote(pb0.at[to], rb0.at[i], sb_sem, rb_sem, 1, to).start()
        report(0, bits_at(0))

    for k in range(1, SEGS):
        pl.when(seg == k)(functools.partial(advance, k))

    @pl.when(seg < last)
    def _():
        wait_bytes(fr, fr_sem)
        answer, _state = early_sites(fr[...])
        out[...] = row_of(answer, 0, slots)

    for k in range(last):
        pl.when(seg == k)(functools.partial(drain, k))

    @pl.when(seg == last)
    def _():
        k, rows = last, 2 ** (last + 1)
        wait_bytes(r0, r0_sem)
        share = s0[...]
        known = jnp.where(iota((1, LANES), 1) < slots, share + total_of(r0, bonds - 1, slice(0, 1)), share)
        fs[...] = known
        for to in range(last):
            remote(fs, fr, f_sem, fr_sem, to, bond).start()
        wait_bytes(rb[k], rb3_sem)
        env = pb[k][zs.index(0) * nx + x_me] + total_of(rb[k], len(sources(k, nz, nx)), slice(0, rows))
        s1[...] = norm_row(env, k)
        to_everyone(s1, r1, s1_sem, r1_sem)
        _answer, state = early_sites(known)
        bit = pick(order_column, jnp.concatenate([bits_row] * (LANES // slots), axis=1))
        wait_bytes(r1, r1_sem)
        norms = s1[...] + total_of(r1, bonds - 1, slice(0, 1))
        probability, *_state = site_probability(k, jnp.broadcast_to(norms, (slots, LANES)), bit, *state)
        out[...] = row_of(probability, 0, slots)
        wait_bytes(r0, s0_sem)
        wait_bytes(r1, s1_sem)
        for _i in range(last):
            wait_bytes(fs, f_sem)
        drain(k)


def on_device(nz, nx, sites, boundary, bits, order):
    slots = bits.shape[0]
    width, dim = sites.shape[2], sites.shape[3]
    f32, i32 = jnp.float32, jnp.int32
    bonds, ng = nz * nx * 2, nx * 2
    rows = [2 ** (k + 1) for k in range(SEGS)]
    pieces = [pltpu.VMEM((nz, nx * rows[k], LANES), f32) for k in range(1, SEGS)]
    sends = [pltpu.VMEM(((nz + unmerged(k, nz)) * nx, rows[k], LANES), f32) for k in range(SEGS)]
    receives = [pltpu.VMEM((len(sources(k, nz, nx)), rows[k], LANES), f32) for k in range(SEGS)]
    one = pltpu.VMEM((1, LANES), f32)
    all_rows = pltpu.VMEM((bonds - 1, 1, LANES), f32)
    dma = pltpu.SemaphoreType.DMA
    scratch = [
        pltpu.VMEM((nz, 2, width, ng * width), f32),
        pltpu.VMEM((nz, 2, 2 * width, 2 * nx * width), jnp.bfloat16),
        pltpu.VMEM((width, LANES), f32),
        pltpu.VMEM((1, width), f32), pltpu.VMEM((1, slots), i32), pltpu.VMEM((1, slots), i32),
        *pieces, *pieces, *sends, *receives,
        one, pltpu.VMEM((SEGS - 1, 1, LANES), f32), one, one, one, all_rows, one, all_rows,
        dma((nz,)), dma((3,)), dma((SEGS - 1,)), dma((nz,)), *([dma(())] * 11),
    ]
    hbm = pl.BlockSpec(memory_space=pltpu.HBM)
    answer = pl.pallas_call(
        functools.partial(kernel, nz, nx, slots, dim),
        out_shape=jax.ShapeDtypeStruct((1, slots), f32),
        in_specs=[hbm] * 4,
        out_specs=pl.BlockSpec(memory_space=pltpu.VMEM),
        scratch_shapes=scratch,
        compiler_params=pltpu.CompilerParams(
            collective_id=0, has_side_effects=True, vmem_limit_bytes=67043328
        ),
        name="chain",
    )(sites, boundary.reshape(1, width), bits.T, order.reshape(1, slots))
    return answer.T


def solution(mesh):
    nz, nx = grouping(mesh.shape["bond"])
    return jax.shard_map(
        functools.partial(on_device, nz, nx),
        mesh=mesh,
        in_specs=(P("seg", None, "bond", None), P("bond"), P(None, "seg"), P()),
        out_specs=P(None, "seg"),
        check_vma=False,
    )
```

```python
import functools

import jax
import jax.numpy as jnp
from jax import lax
from jax.experimental import pallas as pl
from jax.experimental.pallas import tpu as pltpu
from jax.sharding import PartitionSpec as P

EPSILON = 1e-06
LANES = 128
SEGS = 4
MESH = pl.DeviceIdType.MESH
UNMERGED = (8, 3, 1, 0)


def grouping(bonds):
    return (8, 4) if bonds == 64 else (bonds // 2, 1)


def far_first(n):
    return sorted(range(n), key=lambda d: -min(d, n - d))


def unmerged(k, nz):
    return min(UNMERGED[k], nz - 1) if k else nz


def sources(k, nz, nx):
    direct = far_first(nz)[: unmerged(k, nz)]
    listed = [
        (dz, dx, dc) for dz in far_first(nz) for dx in far_first(nx) for dc in ((1, 0) if dz in direct else (0,))
    ]
    if k == SEGS - 1:
        listed.remove((0, 0, 0))
    return listed


def iota(shape, axis):
    return lax.broadcasted_iota(jnp.int32, shape, axis)


def column_of(row, rows):
    shape = (rows, row.shape[1])
    hit = iota(shape, 1) == iota(shape, 0)
    zero = jnp.zeros((), row.dtype)
    return jnp.sum(jnp.where(hit, jnp.broadcast_to(row, shape), zero), axis=1, keepdims=True)


def row_of(column, offset, lanes=LANES):
    shape = (column.shape[0], lanes)
    hit = iota(shape, 1) == iota(shape, 0) + offset
    return jnp.sum(jnp.where(hit, jnp.broadcast_to(column, shape), 0.0), axis=0, keepdims=True)


def total_of(ref, count, rows):
    chains = [ref[i, rows, :] for i in range(min(4, count))]
    for i in range(4, count):
        chains[i % 4] = chains[i % 4] + ref[i, rows, :]
    while len(chains) > 1:
        chains = [sum(chains[i + 1 : i + 2], chains[i]) for i in range(0, len(chains), 2)]
    return chains[0]


def level_offset(k):
    return 2 ** (k + 1) - 2


def kernel(
    nz, nx, slots, dim,
    sites, boundary_hbm, bits_hbm, order_hbm, out,
    tile, tile2, split, env0, boundary, bits, order,
    pp1, pp2, rp1, rp2, halves, pe, re,
    pb0, pb1, pb2, pb3, rb0, rb1, rb2, rb3,
    note, notes, fs, fr, s0, r0, s1, r1,
    load_sem, small_sem, notes_sem, rp_sem, note_sem, sp_sem, sb_sem, rb_sem, rb3_sem, f_sem, fr_sem,
    s0_sem, r0_sem, s1_sem, r1_sem, st_sem, rt_sem, pe_sem, re_sem,
):
    pp, rp = (None, pp1, pp2), (None, rp1, rp2)
    pb, rb = (pb0, pb1, pb2, pb3), (rb0, rb1, rb2, rb3)
    last = SEGS - 1
    bonds, ng = nz * nx * 2, nx * 2
    width = tile.shape[2]
    seg, bond = lax.axis_index("seg"), lax.axis_index("bond")
    z_me, g_me = lax.div(bond, ng), lax.rem(bond, ng)
    x_me, c_me = lax.div(g_me, 2), lax.rem(g_me, 2)
    partner = lax.rem(c_me + 1, 2)
    xs = far_first(nx)
    chips = [(dz, dx) for dz in far_first(nz) for dx in xs]

    def at(dz, dx, core):
        return (lax.rem(z_me + dz, nz) * nx + lax.rem(x_me + dx, nx)) * 2 + core

    def remote(src, dst, send, recv, to_seg, to_bond):
        return pltpu.make_async_remote_copy(
            src_ref=src, dst_ref=dst, send_sem=send, recv_sem=recv,
            device_id={"seg": to_seg, "bond": to_bond}, device_id_type=MESH,
        )

    def wait_bytes(ref, sem):
        pltpu.make_async_copy(ref, ref, sem).wait()

    barrier = pltpu.get_barrier_semaphore()

    def hello(to_seg, to_bond):
        pl.semaphore_signal(barrier, inc=1, device_id={"seg": to_seg, "bond": to_bond}, device_id_type=MESH)

    for k in range(1, SEGS):
        @pl.when(seg == k)
        def _(k=k):
            for dz, dx, dc in sources(k - 1, nz, nx):
                hello(k - 1, at(dz, dx, lax.rem(c_me + dc, 2)))

    everyone = [(dz, dx, dc) for dz, dx in chips for dc in (1, 0) if dz or dx or dc]

    @pl.when(seg == last)
    def _():
        for dz, dx, dc in everyone:
            hello(seg, at(dz, dx, lax.rem(c_me + dc, 2)))
        for k in range(last - 1):
            hello(k, bond)

    @pl.when(seg < last)
    def _():
        hello(last, bond)

    @pl.when(jnp.logical_and(seg > 0, seg < last))
    def _():
        hello(seg, at(0, 0, partner))

    small = [
        pltpu.make_async_copy(src, dst, small_sem.at[i])
        for i, (src, dst) in enumerate(((boundary_hbm, boundary), (bits_hbm, bits), (order_hbm, order)))
    ]
    for copy in small:
        copy.start()

    zs = far_first(nz)

    @pl.loop(0, nz)
    def _(z):
        start = pl.multiple_of(z * ng * width, width)
        pltpu.make_async_copy(sites.at[0, :, :, pl.ds(start, ng * width)], tile.at[z], load_sem.at[z]).start()

    for copy in small:
        copy.wait()
    bits_row = bits[...].astype(jnp.float32)
    order_column = column_of(order[...], slots)

    def bits_at(k):
        parts = [jnp.zeros((1, slots), jnp.float32)] * (LANES // slots)
        parts[k + 1] = bits_row
        return jnp.concatenate(parts, axis=1)

    @pl.when(seg == 0)
    def _():
        env0[...] = jnp.broadcast_to(column_of(boundary[...], width), (width, LANES))

        @pl.loop(0, nz)
        def _(z):
            wait_bytes(tile.at[z], load_sem.at[z])
            for g in range(ng):
                for s in range(2):
                    a = tile[z, s, :, g * width : (g + 1) * width]
                    pb0[z * ng + g, s : s + 1, :] = jnp.sum(a * env0[...], axis=0, keepdims=True)

    def split_into(z, half, s, x, a):
        high = a.astype(jnp.bfloat16)
        low = (a - high.astype(jnp.float32)).astype(jnp.bfloat16)
        column = (s * nx + x) * width
        split[z, half, 0:width, column : column + width] = high
        split[z, half, width : 2 * width, column : column + width] = low

    @pl.when(jnp.logical_and(seg > 0, seg < last))
    def _():
        @pl.loop(0, nz)
        def _(z):
            wait_bytes(tile.at[z], load_sem.at[z])
            for s in range(2):
                for g in range(ng):
                    split_into(z, g % 2, s, g // 2, tile[z, s, :, g * width : (g + 1) * width])

    for k in range(SEGS):
        @pl.when(seg == k)
        def _(k=k):
            if k == last:
                count = len(everyone) + last
            else:
                count = len(sources(k, nz, nx)) + (1 if k > 0 else 0) + (1 if k < last - 1 else 0)
            pl.semaphore_wait(barrier, count)

    @pl.when(seg == last)
    def _():
        @pl.loop(0, nz)
        def _(z):
            wait_bytes(tile.at[z], load_sem.at[z])
            for x in range(nx):
                start = pl.multiple_of((x * 2 + partner) * width, width)
                remote(
                    tile.at[z, :, :, pl.ds(start, width)], tile2.at[z, :, :, pl.ds(x * width, width)],
                    st_sem.at[z], rt_sem.at[z], seg, at(0, 0, partner),
                ).start()

        @pl.loop(0, nz)
        def _(z):
            for s in range(2):
                for x in range(nx):
                    start = pl.multiple_of((x * 2 + c_me) * width, width)
                    split_into(z, 0, s, x, tile[z, s, :, pl.ds(start, width)])

        @pl.loop(0, nz)
        def _(z):
            wait_bytes(tile2.at[z], rt_sem.at[z])
            for s in range(2):
                for x in range(nx):
                    split_into(z, 1, s, x, tile2[z, s, :, x * width : (x + 1) * width])

    lanes = iota((slots, LANES), 1)

    def pick(where_lane, source):
        return jnp.sum(jnp.where(lanes == where_lane, source, 0.0), axis=1, keepdims=True)

    def site_probability(k, table, bit, node, scale):
        chosen = (bit > 0.5).astype(jnp.int32)
        base = level_offset(k) + node
        m_chosen = pick(base + chosen * 2**k, table) / scale + EPSILON
        m_other = pick(base + (1 - chosen) * 2**k, table) / scale + EPSILON
        return m_chosen / (m_chosen + m_other), node + chosen * 2**k, scale * m_chosen

    def early_sites(known):
        table = jnp.broadcast_to(known, (slots, LANES))
        state = (jnp.zeros((slots, 1), jnp.int32), jnp.full((slots, 1), float(dim), jnp.float32))
        answer = jnp.zeros((slots, 1), jnp.float32)
        for k in range(last):
            bit = pick(order_column + slots * (k + 1), table)
            probability, *state = site_probability(k, table, bit, *state)
            answer = jnp.where(seg == k, probability, answer)
        return answer, state

    def receive(k):
        wait_bytes(rb[k - 1], rb_sem)
        return total_of(rb[k - 1], len(sources(k - 1, nz, nx)), slice(0, 2**k))

    def norm_row(env, k):
        return row_of(jnp.sum(env * env, axis=1, keepdims=True), level_offset(k))

    def report(k, row):
        note[...] = row
        remote(note, notes.at[k], note_sem, notes_sem.at[k], last, bond).start()

    def left_of(env):
        rows = env.shape[0]
        if rows < 8:
            env = jnp.concatenate([env, jnp.zeros((8 - rows, width), jnp.float32)], axis=0)
        high = env.astype(jnp.bfloat16).astype(jnp.float32)
        both = jnp.concatenate([high, env - high], axis=0).astype(jnp.bfloat16)
        return jnp.concatenate([both, both], axis=1)

    def advance_last():
        k, rows_in = last, 2**last
        env = receive(k)
        pe[...] = env
        remote(pe, re, pe_sem, re_sem, seg, at(0, 0, partner)).start()
        slot_of = {source: i for i, source in enumerate(sources(k, nz, nx))}

        def half(left, t, which):
            z = lax.rem(z_me + zs[t], nz)
            value = jnp.dot(left, split[z, which], preferred_element_type=jnp.float32)
            return value[0:8] + value[8:16]

        left = left_of(env)
        share = norm_row(env, k - 1)
        for i in range(last):
            wait_bytes(notes.at[i], notes_sem.at[i])
            share = share + notes[i]
        s0[...] = share
        each = -(-len(everyone) // nz)
        for t in range(nz):
            halves[t] = half(left, t, 0)
            to_everyone(s0, r0, s0_sem, r0_sem, t * each, (t + 1) * each)
        wait_bytes(re, re_sem)
        left = left_of(re[...])

        def finish(t, value):
            value = value + halves[t]
            for x in range(nx):
                for s in range(2):
                    column = (s * nx + x) * width
                    pb[k][t * nx + x, s * rows_in : (s + 1) * rows_in, :] = value[:, column : column + width]
            for dx in xs:
                source = (zs[t], dx, 0)
                if source in slot_of:
                    x = lax.rem(x_me + dx, nx)
                    remote(
                        pb[k].at[t * nx + x], rb[k].at[slot_of[source]], sb_sem, rb3_sem, seg, at(zs[t], dx, c_me)
                    ).start()

        held = half(left, 0, 1)
        for t in range(1, nz):
            value = half(left, t, 1)
            finish(t - 1, held)
            held = value
        finish(nz - 1, held)
    def advance(k):
        rows_in, rows_out = 2**k, 2 ** (k + 1)
        env = receive(k)
        left = left_of(env)
        slot_of = {source: i for i, source in enumerate(sources(k, nz, nx))}

        def blocks(t, core):
            z = lax.rem(z_me + zs[t], nz)
            value = jnp.dot(left, split[z, core], preferred_element_type=jnp.float32)
            value = value[0:8] + value[8:16]
            for x in range(nx):
                for s in range(2):
                    column = (s * nx + x) * width
                    yield x, s * rows_in, value[0:rows_in, column : column + width]

        def to_partner(t, products):
            for x, row, value in products:
                row = x * rows_out + row
                pp[k][t, row : row + rows_in, :] = value
            remote(pp[k].at[t], rp[k].at[t], sp_sem, rp_sem.at[t], seg, at(0, 0, partner)).start()

        def send(t, dc, piece_at):
            for dx in xs:
                source = (zs[t], dx, dc)
                if source in slot_of:
                    x = lax.rem(x_me + dx, nx)
                    to = at(zs[t], dx, lax.rem(c_me + dc, 2))
                    remote(pb[k].at[piece_at + x], rb[k].at[slot_of[source]], sb_sem, rb_sem, seg + 1, to).start()

        def own(t, products):
            wait_bytes(rp[k].at[t], rp_sem.at[t])
            for x, row, value in products:
                sent = x * rows_out + row
                pb[k][t * nx + x, row : row + rows_in, :] = value + rp[k][t, sent : sent + rows_in, :]
            send(t, 0, t * nx)

        def direct(dc, t, products):
            piece_at = (t + dc * nz) * nx
            for x, row, value in products:
                pb[k][piece_at + x, row : row + rows_in, :] = value
            send(t, dc, piece_at)

        far = unmerged(k, nz)
        both_cores = [(functools.partial(direct, dc), t, (c_me, partner)[dc]) for t in range(far) for dc in (1, 0)]
        exchanged = [(to_partner, t, partner) for t in range(far, nz)]
        steps = both_cores[:2] + exchanged[:2] + both_cores[2:] + exchanged[2:]
        steps += [(own, t, c_me) for t in range(far, nz)]
        held = None
        for finish, t, core in steps:
            products = list(blocks(t, core))
            if held is not None:
                held[0](*held[1:])
            held = (finish, t, products)
        held[0](*held[1:])
        report(k, norm_row(env, k - 1) + bits_at(k))

    def to_everyone(src, dst, send, recv, start=0, stop=None):
        for i, (dz, dx, dc) in list(enumerate(everyone))[start:stop]:
            remote(src, dst.at[i], send, recv, seg, at(dz, dx, lax.rem(c_me + dc, 2))).start()

    def drain(k):
        if k == last:
            wait_bytes(pe, pe_sem)
            for z in range(nz):
                wait_bytes(tile2.at[z], st_sem.at[z])
        elif k:
            far = unmerged(k, nz)
            wait_bytes(rp[k].at[pl.ds(far, nz - far)], sp_sem)
        wait_bytes(rb[k], sb_sem)
        if k < last:
            wait_bytes(note, note_sem)

    @pl.when(seg == 0)
    def _():
        for i, (dz, dx, dc) in enumerate(sources(0, nz, nx)):
            to = at(dz, dx, lax.rem(c_me + dc, 2))
            remote(pb0.at[to], rb0.at[i], sb_sem, rb_sem, 1, to).start()
        report(0, bits_at(0))

    for k in range(1, last):
        pl.when(seg == k)(functools.partial(advance, k))
    pl.when(seg == last)(advance_last)

    @pl.when(seg < last)
    def _():
        wait_bytes(fr, fr_sem)
        answer, _state = early_sites(fr[...])
        out[...] = row_of(answer, 0, slots)

    for k in range(last):
        pl.when(seg == k)(functools.partial(drain, k))

    @pl.when(seg == last)
    def _():
        k, rows = last, 2 ** (last + 1)
        wait_bytes(r0, r0_sem)
        share = s0[...]
        known = jnp.where(iota((1, LANES), 1) < slots, share + total_of(r0, bonds - 1, slice(0, 1)), share)
        fs[...] = known
        for to in range(last):
            remote(fs, fr, f_sem, fr_sem, to, bond).start()
        wait_bytes(rb[k], rb3_sem)
        env = pb[k][zs.index(0) * nx + x_me] + total_of(rb[k], len(sources(k, nz, nx)), slice(0, rows))
        s1[...] = norm_row(env, k)
        to_everyone(s1, r1, s1_sem, r1_sem)
        _answer, state = early_sites(known)
        bit = pick(order_column, jnp.concatenate([bits_row] * (LANES // slots), axis=1))
        wait_bytes(r1, r1_sem)
        norms = s1[...] + total_of(r1, bonds - 1, slice(0, 1))
        probability, *_state = site_probability(k, jnp.broadcast_to(norms, (slots, LANES)), bit, *state)
        out[...] = row_of(probability, 0, slots)
        wait_bytes(r0, s0_sem)
        wait_bytes(r1, s1_sem)
        for _i in range(last):
            wait_bytes(fs, f_sem)
        drain(k)


def on_device(nz, nx, sites, boundary, bits, order):
    slots = bits.shape[0]
    width, dim = sites.shape[2], sites.shape[3]
    f32, i32 = jnp.float32, jnp.int32
    bonds, ng = nz * nx * 2, nx * 2
    rows = [2 ** (k + 1) for k in range(SEGS)]
    pieces = [pltpu.VMEM((nz, nx * rows[k], LANES), f32) for k in range(1, SEGS - 1)]
    sends = [pltpu.VMEM(((nz + unmerged(k, nz)) * nx, rows[k], LANES), f32) for k in range(SEGS)]
    receives = [pltpu.VMEM((len(sources(k, nz, nx)), rows[k], LANES), f32) for k in range(SEGS)]
    one = pltpu.VMEM((1, LANES), f32)
    all_rows = pltpu.VMEM((bonds - 1, 1, LANES), f32)
    dma = pltpu.SemaphoreType.DMA
    scratch = [
        pltpu.VMEM((nz, 2, width, ng * width), f32),
        pltpu.VMEM((nz, 2, width, nx * width), f32),
        pltpu.VMEM((nz, 2, 2 * width, 2 * nx * width), jnp.bfloat16),
        pltpu.VMEM((width, LANES), f32),
        pltpu.VMEM((1, width), f32), pltpu.VMEM((1, slots), i32), pltpu.VMEM((1, slots), i32),
        *pieces, *pieces, pltpu.VMEM((nz, 8, 2 * nx * width), f32), pltpu.VMEM((8, LANES), f32), pltpu.VMEM((8, LANES), f32),
        *sends, *receives,
        one, pltpu.VMEM((SEGS - 1, 1, LANES), f32), one, one, one, all_rows, one, all_rows,
        dma((nz,)), dma((3,)), dma((SEGS - 1,)), dma((nz,)), *([dma(())] * 11), dma((nz,)), dma((nz,)), dma(()), dma(()),
    ]
    hbm = pl.BlockSpec(memory_space=pltpu.HBM)
    answer = pl.pallas_call(
        functools.partial(kernel, nz, nx, slots, dim),
        out_shape=jax.ShapeDtypeStruct((1, slots), f32),
        in_specs=[hbm] * 4,
        out_specs=pl.BlockSpec(memory_space=pltpu.VMEM),
        scratch_shapes=scratch,
        compiler_params=pltpu.CompilerParams(
            collective_id=0, has_side_effects=True, vmem_limit_bytes=67043328
        ),
        name="chain",
    )(sites, boundary.reshape(1, width), bits.T, order.reshape(1, slots))
    return answer.T


def solution(mesh):
    nz, nx = grouping(mesh.shape["bond"])
    return jax.shard_map(
        functools.partial(on_device, nz, nx),
        mesh=mesh,
        in_specs=(P("seg", None, "bond", None), P("bond"), P(None, "seg"), P()),
        out_specs=P(None, "seg"),
        check_vma=False,
    )
```

```python
import functools

import jax
import jax.numpy as jnp
from jax import lax
from jax.experimental import pallas as pl
from jax.experimental.pallas import tpu as pltpu
from jax.sharding import PartitionSpec as P

EPSILON = 1e-06
LANES = 128
SEGS = 4
MESH = pl.DeviceIdType.MESH
UNMERGED = (8, 3, 1, 0)


def grouping(bonds):
    return (8, 4) if bonds == 64 else (bonds // 2, 1)


def far_first(n):
    return sorted(range(n), key=lambda d: -min(d, n - d))


def unmerged(k, nz):
    return min(UNMERGED[k], nz - 1) if k else nz


def sources(k, nz, nx):
    direct = far_first(nz)[: unmerged(k, nz)]
    listed = [
        (dz, dx, dc) for dz in far_first(nz) for dx in far_first(nx) for dc in ((1, 0) if dz in direct else (0,))
    ]
    if k == SEGS - 1:
        listed.remove((0, 0, 0))
    return listed


def iota(shape, axis):
    return lax.broadcasted_iota(jnp.int32, shape, axis)


def column_of(row, rows):
    shape = (rows, row.shape[1])
    hit = iota(shape, 1) == iota(shape, 0)
    zero = jnp.zeros((), row.dtype)
    return jnp.sum(jnp.where(hit, jnp.broadcast_to(row, shape), zero), axis=1, keepdims=True)


def row_of(column, offset, lanes=LANES):
    shape = (column.shape[0], lanes)
    hit = iota(shape, 1) == iota(shape, 0) + offset
    return jnp.sum(jnp.where(hit, jnp.broadcast_to(column, shape), 0.0), axis=0, keepdims=True)


def total_of(ref, count, rows):
    chains = [ref[i, rows, :] for i in range(min(4, count))]
    for i in range(4, count):
        chains[i % 4] = chains[i % 4] + ref[i, rows, :]
    while len(chains) > 1:
        chains = [sum(chains[i + 1 : i + 2], chains[i]) for i in range(0, len(chains), 2)]
    return chains[0]


def level_offset(k):
    return 2 ** (k + 1) - 2


def kernel(
    nz, nx, slots, dim,
    sites, boundary_hbm, bits_hbm, order_hbm, out,
    tile, tile2, split, env0, boundary, bits, order,
    pp1, pp2, rp1, rp2, halves, pe, re,
    pb0, pb1, pb2, pb3, rb0, rb1, rb2, rb3,
    note, notes, fs, fr, s0, r0, s1, r1,
    load_sem, small_sem, notes_sem, rp_sem, note_sem, sp_sem, sb_sem, rb_sem, rb3_sem, f_sem, fr_sem,
    s0_sem, r0_sem, s1_sem, r1_sem, st_sem, rt_sem, pe_sem, re_sem,
):
    pp, rp = (None, pp1, pp2), (None, rp1, rp2)
    pb, rb = (pb0, pb1, pb2, pb3), (rb0, rb1, rb2, rb3)
    last = SEGS - 1
    bonds, ng = nz * nx * 2, nx * 2
    width = tile.shape[2]
    seg, bond = lax.axis_index("seg"), lax.axis_index("bond")
    z_me, g_me = lax.div(bond, ng), lax.rem(bond, ng)
    x_me, c_me = lax.div(g_me, 2), lax.rem(g_me, 2)
    partner = lax.rem(c_me + 1, 2)
    xs = far_first(nx)
    chips = [(dz, dx) for dz in far_first(nz) for dx in xs]

    def at(dz, dx, core):
        return (lax.rem(z_me + dz, nz) * nx + lax.rem(x_me + dx, nx)) * 2 + core

    def remote(src, dst, send, recv, to_seg, to_bond):
        return pltpu.make_async_remote_copy(
            src_ref=src, dst_ref=dst, send_sem=send, recv_sem=recv,
            device_id={"seg": to_seg, "bond": to_bond}, device_id_type=MESH,
        )

    def wait_bytes(ref, sem):
        pltpu.make_async_copy(ref, ref, sem).wait()

    barrier = pltpu.get_barrier_semaphore()

    def hello(to_seg, to_bond):
        pl.semaphore_signal(barrier, inc=1, device_id={"seg": to_seg, "bond": to_bond}, device_id_type=MESH)

    for k in range(1, SEGS):
        @pl.when(seg == k)
        def _(k=k):
            for dz, dx, dc in sources(k - 1, nz, nx):
                hello(k - 1, at(dz, dx, lax.rem(c_me + dc, 2)))

    everyone = [(dz, dx, dc) for dz, dx in chips for dc in (1, 0) if dz or dx or dc]

    @pl.when(seg == last)
    def _():
        for dz, dx, dc in everyone:
            hello(seg, at(dz, dx, lax.rem(c_me + dc, 2)))
        for k in range(last - 1):
            hello(k, bond)

    @pl.when(seg < last)
    def _():
        hello(last, bond)

    @pl.when(jnp.logical_and(seg > 0, seg < last))
    def _():
        hello(seg, at(0, 0, partner))

    small = [
        pltpu.make_async_copy(src, dst, small_sem.at[i])
        for i, (src, dst) in enumerate(((boundary_hbm, boundary), (bits_hbm, bits), (order_hbm, order)))
    ]
    for copy in small:
        copy.start()

    zs = far_first(nz)

    @pl.loop(0, nz)
    def _(z):
        start = pl.multiple_of(z * ng * width, width)
        pltpu.make_async_copy(sites.at[0, :, :, pl.ds(start, ng * width)], tile.at[z], load_sem.at[z]).start()

    for copy in small:
        copy.wait()
    bits_row = bits[...].astype(jnp.float32)
    order_column = column_of(order[...], slots)

    def bits_at(k):
        parts = [jnp.zeros((1, slots), jnp.float32)] * (LANES // slots)
        parts[k + 1] = bits_row
        return jnp.concatenate(parts, axis=1)

    @pl.when(seg == 0)
    def _():
        env0[...] = jnp.broadcast_to(column_of(boundary[...], width), (width, LANES))

        @pl.loop(0, nz)
        def _(z):
            wait_bytes(tile.at[z], load_sem.at[z])
            for g in range(ng):
                for s in range(2):
                    a = tile[z, s, :, g * width : (g + 1) * width]
                    pb0[z * ng + g, s : s + 1, :] = jnp.sum(a * env0[...], axis=0, keepdims=True)

    def split_into(z, half, s, x, a):
        high = a.astype(jnp.bfloat16)
        low = (a - high.astype(jnp.float32)).astype(jnp.bfloat16)
        column = (s * nx + x) * width
        split[z, half, 0:width, column : column + width] = high
        split[z, half, width : 2 * width, column : column + width] = low

    @pl.when(jnp.logical_and(seg > 0, seg < last))
    def _():
        @pl.loop(0, nz)
        def _(z):
            wait_bytes(tile.at[z], load_sem.at[z])
            for s in range(2):
                for g in range(ng):
                    split_into(z, g % 2, s, g // 2, tile[z, s, :, g * width : (g + 1) * width])

    for k in range(SEGS):
        @pl.when(seg == k)
        def _(k=k):
            if k == last:
                count = len(everyone) + last
            else:
                count = len(sources(k, nz, nx)) + (1 if k > 0 else 0) + (1 if k < last - 1 else 0)
            pl.semaphore_wait(barrier, count)

    @pl.when(seg == last)
    def _():
        @pl.loop(0, nz)
        def _(z):
            wait_bytes(tile.at[z], load_sem.at[z])
            for x in range(nx):
                start = pl.multiple_of((x * 2 + partner) * width, width)
                remote(
                    tile.at[z, :, :, pl.ds(start, width)], tile2.at[z, :, :, pl.ds(x * width, width)],
                    st_sem.at[z], rt_sem.at[z], seg, at(0, 0, partner),
                ).start()

        @pl.loop(0, nz)
        def _(z):
            for s in range(2):
                for x in range(nx):
                    start = pl.multiple_of((x * 2 + c_me) * width, width)
                    split_into(z, 0, s, x, tile[z, s, :, pl.ds(start, width)])

        @pl.loop(0, nz)
        def _(z):
            wait_bytes(tile2.at[z], rt_sem.at[z])
            for s in range(2):
                for x in range(nx):
                    split_into(z, 1, s, x, tile2[z, s, :, x * width : (x + 1) * width])

    lanes = iota((slots, LANES), 1)

    def pick(where_lane, source):
        return jnp.sum(jnp.where(lanes == where_lane, source, 0.0), axis=1, keepdims=True)

    def site_probability(k, table, bit, node, scale):
        chosen = (bit > 0.5).astype(jnp.int32)
        base = level_offset(k) + node
        m_chosen = pick(base + chosen * 2**k, table) / scale + EPSILON
        m_other = pick(base + (1 - chosen) * 2**k, table) / scale + EPSILON
        return m_chosen / (m_chosen + m_other), node + chosen * 2**k, scale * m_chosen

    def early_sites(known):
        table = jnp.broadcast_to(known, (slots, LANES))
        state = (jnp.zeros((slots, 1), jnp.int32), jnp.full((slots, 1), float(dim), jnp.float32))
        answer = jnp.zeros((slots, 1), jnp.float32)
        for k in range(last):
            bit = pick(order_column + slots * (k + 1), table)
            probability, *state = site_probability(k, table, bit, *state)
            answer = jnp.where(seg == k, probability, answer)
        return answer, state

    def receive(k):
        wait_bytes(rb[k - 1], rb_sem)
        return total_of(rb[k - 1], len(sources(k - 1, nz, nx)), slice(0, 2**k))

    def norm_row(env, k):
        return row_of(jnp.sum(env * env, axis=1, keepdims=True), level_offset(k))

    def report(k, row):
        note[...] = row
        remote(note, notes.at[k], note_sem, notes_sem.at[k], last, bond).start()

    def left_of(env):
        rows = env.shape[0]
        if rows < 8:
            env = jnp.concatenate([env, jnp.zeros((8 - rows, width), jnp.float32)], axis=0)
        high = env.astype(jnp.bfloat16).astype(jnp.float32)
        both = jnp.concatenate([high, env - high], axis=0).astype(jnp.bfloat16)
        return jnp.concatenate([both, both], axis=1)

    def advance_last():
        k, rows_in = last, 2**last
        env = receive(k)
        pe[...] = env
        remote(pe, re, pe_sem, re_sem, seg, at(0, 0, partner)).start()
        slot_of = {source: i for i, source in enumerate(sources(k, nz, nx))}

        def half(left, t, which):
            z = lax.rem(z_me + zs[t], nz)
            value = jnp.dot(left, split[z, which], preferred_element_type=jnp.float32)
            return value[0:8] + value[8:16]

        left = left_of(env)
        share = norm_row(env, k - 1)
        for i in range(last):
            wait_bytes(notes.at[i], notes_sem.at[i])
            share = share + notes[i]
        s0[...] = share
        each = -(-len(everyone) // nz)
        for t in range(nz):
            halves[t] = half(left, t, 0)
            to_everyone(s0, r0, s0_sem, r0_sem, t * each, (t + 1) * each)
        wait_bytes(re, re_sem)
        left = left_of(re[...])

        def finish(t, value):
            value = value + halves[t]
            for x in range(nx):
                for s in range(2):
                    column = (s * nx + x) * width
                    pb[k][t * nx + x, s * rows_in : (s + 1) * rows_in, :] = value[:, column : column + width]
            for dx in xs:
                source = (zs[t], dx, 0)
                if source in slot_of:
                    x = lax.rem(x_me + dx, nx)
                    remote(
                        pb[k].at[t * nx + x], rb[k].at[slot_of[source]], sb_sem, rb3_sem, seg, at(zs[t], dx, c_me)
                    ).start()

        held = half(left, 0, 1)
        for t in range(1, nz):
            value = half(left, t, 1)
            finish(t - 1, held)
            held = value
        finish(nz - 1, held)
    def advance(k):
        rows_in, rows_out = 2**k, 2 ** (k + 1)
        env = receive(k)
        left = left_of(env)
        slot_of = {source: i for i, source in enumerate(sources(k, nz, nx))}

        def blocks(t, core):
            z = lax.rem(z_me + zs[t], nz)
            value = jnp.dot(left, split[z, core], preferred_element_type=jnp.float32)
            value = value[0:8] + value[8:16]
            for x in range(nx):
                for s in range(2):
                    column = (s * nx + x) * width
                    yield x, s * rows_in, value[0:rows_in, column : column + width]

        def to_partner(t, products):
            for x, row, value in products:
                row = x * rows_out + row
                pp[k][t, row : row + rows_in, :] = value
            remote(pp[k].at[t], rp[k].at[t], sp_sem, rp_sem.at[t], seg, at(0, 0, partner)).start()

        def send(t, dc, piece_at):
            for dx in xs:
                source = (zs[t], dx, dc)
                if source in slot_of:
                    x = lax.rem(x_me + dx, nx)
                    to = at(zs[t], dx, lax.rem(c_me + dc, 2))
                    remote(pb[k].at[piece_at + x], rb[k].at[slot_of[source]], sb_sem, rb_sem, seg + 1, to).start()

        def own(t, products):
            wait_bytes(rp[k].at[t], rp_sem.at[t])
            for x, row, value in products:
                sent = x * rows_out + row
                pb[k][t * nx + x, row : row + rows_in, :] = value + rp[k][t, sent : sent + rows_in, :]
            send(t, 0, t * nx)

        def direct(dc, t, products):
            piece_at = (t + dc * nz) * nx
            for x, row, value in products:
                pb[k][piece_at + x, row : row + rows_in, :] = value
            send(t, dc, piece_at)

        far = unmerged(k, nz)
        both_cores = [(functools.partial(direct, dc), t, (c_me, partner)[dc]) for t in range(far) for dc in (1, 0)]
        exchanged = [(to_partner, t, partner) for t in range(far, nz)]
        steps = exchanged[:2] + both_cores + exchanged[2:]
        steps += [(own, t, c_me) for t in range(far, nz)]
        held = None
        for finish, t, core in steps:
            products = list(blocks(t, core))
            if held is not None:
                held[0](*held[1:])
            held = (finish, t, products)
        held[0](*held[1:])
        report(k, norm_row(env, k - 1) + bits_at(k))

    def to_everyone(src, dst, send, recv, start=0, stop=None):
        for i, (dz, dx, dc) in list(enumerate(everyone))[start:stop]:
            remote(src, dst.at[i], send, recv, seg, at(dz, dx, lax.rem(c_me + dc, 2))).start()

    def drain(k):
        if k == last:
            wait_bytes(pe, pe_sem)
            for z in range(nz):
                wait_bytes(tile2.at[z], st_sem.at[z])
        elif k:
            far = unmerged(k, nz)
            wait_bytes(rp[k].at[pl.ds(far, nz - far)], sp_sem)
        wait_bytes(rb[k], sb_sem)
        if k < last:
            wait_bytes(note, note_sem)

    @pl.when(seg == 0)
    def _():
        for i, (dz, dx, dc) in enumerate(sources(0, nz, nx)):
            to = at(dz, dx, lax.rem(c_me + dc, 2))
            remote(pb0.at[to], rb0.at[i], sb_sem, rb_sem, 1, to).start()
        report(0, bits_at(0))

    for k in range(1, last):
        pl.when(seg == k)(functools.partial(advance, k))
    pl.when(seg == last)(advance_last)

    @pl.when(seg < last)
    def _():
        wait_bytes(fr, fr_sem)
        answer, _state = early_sites(fr[...])
        out[...] = row_of(answer, 0, slots)

    for k in range(last):
        pl.when(seg == k)(functools.partial(drain, k))

    @pl.when(seg == last)
    def _():
        k, rows = last, 2 ** (last + 1)
        wait_bytes(r0, r0_sem)
        share = s0[...]
        known = jnp.where(iota((1, LANES), 1) < slots, share + total_of(r0, bonds - 1, slice(0, 1)), share)
        fs[...] = known
        for to in range(last):
            remote(fs, fr, f_sem, fr_sem, to, bond).start()
        wait_bytes(rb[k], rb3_sem)
        env = pb[k][zs.index(0) * nx + x_me] + total_of(rb[k], len(sources(k, nz, nx)), slice(0, rows))
        s1[...] = norm_row(env, k)
        to_everyone(s1, r1, s1_sem, r1_sem)
        _answer, state = early_sites(known)
        bit = pick(order_column, jnp.concatenate([bits_row] * (LANES // slots), axis=1))
        wait_bytes(r1, r1_sem)
        norms = s1[...] + total_of(r1, bonds - 1, slice(0, 1))
        probability, *_state = site_probability(k, jnp.broadcast_to(norms, (slots, LANES)), bit, *state)
        out[...] = row_of(probability, 0, slots)
        wait_bytes(r0, s0_sem)
        wait_bytes(r1, s1_sem)
        for _i in range(last):
            wait_bytes(fs, f_sem)
        drain(k)


def on_device(nz, nx, sites, boundary, bits, order):
    slots = bits.shape[0]
    width, dim = sites.shape[2], sites.shape[3]
    f32, i32 = jnp.float32, jnp.int32
    bonds, ng = nz * nx * 2, nx * 2
    rows = [2 ** (k + 1) for k in range(SEGS)]
    pieces = [pltpu.VMEM((nz, nx * rows[k], LANES), f32) for k in range(1, SEGS - 1)]
    sends = [pltpu.VMEM(((nz + unmerged(k, nz)) * nx, rows[k], LANES), f32) for k in range(SEGS)]
    receives = [pltpu.VMEM((len(sources(k, nz, nx)), rows[k], LANES), f32) for k in range(SEGS)]
    one = pltpu.VMEM((1, LANES), f32)
    all_rows = pltpu.VMEM((bonds - 1, 1, LANES), f32)
    dma = pltpu.SemaphoreType.DMA
    scratch = [
        pltpu.VMEM((nz, 2, width, ng * width), f32),
        pltpu.VMEM((nz, 2, width, nx * width), f32),
        pltpu.VMEM((nz, 2, 2 * width, 2 * nx * width), jnp.bfloat16),
        pltpu.VMEM((width, LANES), f32),
        pltpu.VMEM((1, width), f32), pltpu.VMEM((1, slots), i32), pltpu.VMEM((1, slots), i32),
        *pieces, *pieces, pltpu.VMEM((nz, 8, 2 * nx * width), f32), pltpu.VMEM((8, LANES), f32), pltpu.VMEM((8, LANES), f32),
        *sends, *receives,
        one, pltpu.VMEM((SEGS - 1, 1, LANES), f32), one, one, one, all_rows, one, all_rows,
        dma((nz,)), dma((3,)), dma((SEGS - 1,)), dma((nz,)), *([dma(())] * 11), dma((nz,)), dma((nz,)), dma(()), dma(()),
    ]
    hbm = pl.BlockSpec(memory_space=pltpu.HBM)
    answer = pl.pallas_call(
        functools.partial(kernel, nz, nx, slots, dim),
        out_shape=jax.ShapeDtypeStruct((1, slots), f32),
        in_specs=[hbm] * 4,
        out_specs=pl.BlockSpec(memory_space=pltpu.VMEM),
        scratch_shapes=scratch,
        compiler_params=pltpu.CompilerParams(
            collective_id=0, has_side_effects=True, vmem_limit_bytes=67043328
        ),
        name="chain",
    )(sites, boundary.reshape(1, width), bits.T, order.reshape(1, slots))
    return answer.T


def solution(mesh):
    nz, nx = grouping(mesh.shape["bond"])
    return jax.shard_map(
        functools.partial(on_device, nz, nx),
        mesh=mesh,
        in_specs=(P("seg", None, "bond", None), P("bond"), P(None, "seg"), P()),
        out_specs=P(None, "seg"),
        check_vma=False,
    )
```
